512 devices in a mesh: leaf: 32 (over x, y, core), blk: 16 (over z).
Axes of the slice: x: 4, y: 4, z: 16, core: 2. Of those that a mesh axis runs over, the one named last changes fastest.
Arguments:
- points: float32 [3, 131072], P(None, ('leaf', 'blk')), may hold values from 0 to 1
- iterate: bfloat16 [131072, 256], P(('leaf', 'blk')), may hold values from -6 to 6
- right_side: float32 [131072, 256], P(('leaf', 'blk')), may hold values from -6 to 6
- near_mask: int32 [512, 16], P(('leaf', 'blk')), may hold values from 0 to 1, as said below
- leaf_inverse: bfloat16 [512, 256, 256], P(('leaf', 'blk'))
- skeleton: int32 [3, 32, 512], P(None, 'leaf'), may hold values from 0 to 4095, as said below
- coupling: bfloat16 [3, 32, 512, 512], P(None, 'leaf'), may hold values from -0.25 to 0.25
- reduced_inverse: bfloat16 [3, 32, 512, 512], P(None, 'leaf')
- lift: bfloat16 [3, 131072, 512], P(None, ('leaf', 'blk')), may hold values from -0.25 to 0.25
Outputs:
- correction: float32 [131072, 256], P(('leaf', 'blk'))
The draws below stay inside these ranges and needn't reach their ends.
Inputs may be any that keep to these rules, and one draw needn't show every extreme that they name: near_mask[i, i mod 16] is 1. `skeleton`: the 512 indices of one level and subtree are distinct.
All inputs are finite; a program needn't handle non-finite values.
Results may differ from the reference program's by a relative error of at most 0.014.
Values may be sent and summed in bfloat16 or wider, within the bound.
No kernel may reach another device: no remote copies, remote signals or barrier semaphores. Data moves between devices by JAX's collectives and lax.ppermute only.
A program may use at most 64 MiB of HBM per device.

```python
import math
import jax
import jax.numpy as jnp
from jax import lax

P_SIZE = 256
S = 512
R = 256
LEVELS = 3
NB = 16
SUBTREES = 32
SUB_PTS = 4096
TILES = 512
NPTS = 131072


def draw_near_mask(key, part):
    dens_key, flip_key = jax.random.split(key)
    density = jax.random.randint(dens_key, (TILES, 1), 1, 9)
    rolls = jax.random.randint(flip_key, (TILES, NB), 0, 8)
    chosen = (rolls < density).astype(jnp.int32)
    own_tile = jnp.arange(TILES, dtype=jnp.int32)[:, None] % NB == jnp.arange(NB, dtype=jnp.int32)[None, :]
    return jnp.where(own_tile, 1, chosen).astype(jnp.int32)


def draw_leaf_inverse(key, part):
    noise = jax.random.normal(key, (TILES, P_SIZE, P_SIZE), jnp.float32) * (0.5 / math.sqrt(P_SIZE))
    return (noise + jnp.eye(P_SIZE, dtype=jnp.float32)[None]).astype(jnp.bfloat16)


def draw_reduced_inverse(key, part):
    noise = jax.random.normal(key, (LEVELS, SUBTREES, S, S), jnp.float32) * (0.5 / math.sqrt(S))
    return (noise + jnp.eye(S, dtype=jnp.float32)[None, None]).astype(jnp.bfloat16)


def draw_skeleton(key, part):
    keys = jax.random.split(key, LEVELS * SUBTREES)
    chosen = jax.vmap(lambda single: jax.random.permutation(single, SUB_PTS)[:S])(keys)
    return chosen.reshape(LEVELS, SUBTREES, S).astype(jnp.int32)


def level_of(key, dims, cuts, low, top_value):
    level, own = 1.0, jax.random.fold_in(key, 6)
    for position, shards_of in cuts:
        steps = jnp.exp(jax.random.uniform(jax.random.fold_in(own, position), (shards_of,), jnp.float32, low / len(cuts), top_value / len(cuts)))
        level = level * jnp.repeat(steps, dims[position] // shards_of).reshape([-1 if axis == position else 1 for axis in range(len(dims))])
    return level


def bell_draw(own_key, dims, deviation, limit, shards=(), kind=jnp.bfloat16):
    factor_of = level_of(own_key, dims, shards, -0.22, 0.18) if shards else 1.0
    result = jax.random.normal(own_key, dims, jnp.float32) * deviation * factor_of
    return jnp.minimum(jnp.maximum(result, -limit), limit).astype(kind)


def setup_inputs(seed: int = 0) -> dict:
    seeds = jax.random.split(jax.random.key(seed), 10)
    points = jnp.clip(1.0 * jax.random.uniform(seeds[0], (3, NPTS), jnp.float32) ** level_of(seeds[0], (3, NPTS), ((1, 512),), -0.2, 0.2), 0.0, 1.0)
    iterate = bell_draw(seeds[1], (NPTS, R), 1.0, 6.0, ((0, 512),))
    right_side = bell_draw(seeds[2], (NPTS, R), 1.0, 6.0, ((0, 512),), jnp.float32)
    near_mask = draw_near_mask(jax.random.fold_in(seeds[9], 71), 0)
    leaf_inverse = draw_leaf_inverse(jax.random.fold_in(seeds[9], 71), 0)
    skeleton = draw_skeleton(jax.random.fold_in(seeds[9], 71), 0)
    coupling = bell_draw(seeds[6], (LEVELS, SUBTREES, S, S), S ** -0.5, 0.25, ((1, 32),))
    reduced_inverse = draw_reduced_inverse(jax.random.fold_in(seeds[9], 71), 0)
    lift = bell_draw(seeds[8], (LEVELS, NPTS, S), S ** -0.5, 0.25, ((1, 512),))
    return {"points": points, "iterate": iterate, "right_side": right_side, "near_mask": near_mask, "leaf_inverse": leaf_inverse, "skeleton": skeleton, "coupling": coupling, "reduced_inverse": reduced_inverse, "lift": lift}


kernel_scale = 0.125
spread_coef = 4.0
shift_value = 1.0


def kernel_block(left, right):
    dist = jnp.zeros((left.shape[1], right.shape[1]), jnp.float32)
    for axis_no in range(3):
        diff = left[axis_no][:, None] - right[axis_no][None, :]
        dist = dist + diff * diff
    return kernel_scale * jnp.exp(-spread_coef * dist)


def reduced_solve(args):
    cpl, inverse, own_total, other_total = args
    rhs = own_total - jnp.dot(cpl, other_total.astype(jnp.bfloat16), preferred_element_type=jnp.float32)
    return jnp.dot(inverse, rhs.astype(jnp.bfloat16), preferred_element_type=jnp.float32)


def reference(points, iterate, right_side, near_mask, leaf_inverse, skeleton, coupling, reduced_inverse, lift):
    def near_tile(tile_no):
        group = tile_no // NB
        own_pts = lax.dynamic_slice_in_dim(points, tile_no * P_SIZE, P_SIZE, 1)
        group_pts = lax.dynamic_slice_in_dim(points, group * SUB_PTS, SUB_PTS, 1)
        group_rows = lax.dynamic_slice_in_dim(iterate, group * SUB_PTS, SUB_PTS, 0)
        kernel = kernel_block(own_pts, group_pts).astype(jnp.bfloat16)
        col_mask = jnp.repeat(near_mask[tile_no], P_SIZE).astype(jnp.bfloat16)
        near = jnp.dot(kernel * col_mask[None, :], group_rows, preferred_element_type=jnp.float32)
        own_rhs = lax.dynamic_slice_in_dim(right_side, tile_no * P_SIZE, P_SIZE, 0)
        own_iter = lax.dynamic_slice_in_dim(iterate, tile_no * P_SIZE, P_SIZE, 0)
        resid = own_rhs - shift_value * own_iter.astype(jnp.float32) - near
        return jnp.dot(leaf_inverse[tile_no], resid.astype(jnp.bfloat16), preferred_element_type=jnp.float32)

    solved = lax.map(near_tile, jnp.arange(TILES, dtype=jnp.int32))
    field = solved.reshape(SUBTREES, SUB_PTS, R)
    for level_no in range(LEVELS):
        picked = jax.vmap(lambda rows, index: jnp.take(rows, index, axis=0))(field, skeleton[level_no])
        group_width = 2 ** level_no
        node = picked.reshape(SUBTREES // group_width, group_width, S, R).sum(axis=1)
        node = jnp.repeat(node, group_width, axis=0)
        other = node.reshape(SUBTREES // (2 * group_width), 2, group_width, S, R)[:, ::-1].reshape(SUBTREES, S, R)
        answer = lax.map(reduced_solve, (coupling[level_no], reduced_inverse[level_no], node, other))
        lift_level = lift[level_no].reshape(SUBTREES, SUB_PTS, S)

        def apply_lift(args):
            lift_rows, answer_rows = args
            return jnp.dot(lift_rows, answer_rows.astype(jnp.bfloat16), preferred_element_type=jnp.float32)

        field = field - lax.map(apply_lift, (lift_level, answer))
    return field.reshape(NPTS, R)
```

```python
import math

import jax
import jax.numpy as jnp
from jax import lax
from jax.experimental import pallas as pl
from jax.experimental.pallas import tpu as pltpu
from jax.sharding import PartitionSpec as P

LEVELS = 3
CELL = 4

kernel_scale = 0.125
spread_coef = 4.0
shift_value = 1.0

EXTRA = 8
OFF_BIAS = 30000.0
EXP2_COEF = spread_coef * math.log2(math.e)
EXP2_BASE = math.log2(kernel_scale)

F32 = jnp.float32
BF16 = jnp.bfloat16
VMEM = pl.BlockSpec(memory_space=pltpu.VMEM)
SMEM = pl.BlockSpec(memory_space=pltpu.SMEM)


def dot_nt(left, right):
    return lax.dot_general(left, right, (((1,), (1,)), ((), ())), preferred_element_type=F32)


def dot_tn(left, right):
    return lax.dot_general(left, right, (((0,), (0,)), ((), ())), preferred_element_type=F32)


def dot_nn(left, right):
    return jnp.dot(left, right, preferred_element_type=F32)


def split_parts(value):
    high = value.astype(BF16).astype(F32)
    rest = value - high
    mid = rest.astype(BF16).astype(F32)
    return high, mid, (rest - mid).astype(BF16).astype(F32)


def pack_kernel(points_ref, iterate_ref, mask_ref, out_ref, extra_ref):
    count, rows, pts = out_ref.shape
    block = rows - EXTRA
    point = points_ref[...]
    high = point.astype(BF16).astype(F32)
    extra_ref[...] = jnp.zeros_like(extra_ref)
    extra_ref[0:3, :] = high
    extra_ref[3:4, 0 : mask_ref.shape[1]] = mask_ref[...].astype(F32)
    extra_ref[4:7, :] = point - high
    turned = iterate_ref[...].astype(F32).T.astype(BF16)
    extra = extra_ref[...].astype(BF16)
    for dest in range(count):
        part = dest % CELL
        out_ref[dest, 0:block, :] = turned[part * block : (part + 1) * block]
        out_ref[dest, block:rows, :] = extra


def near_kernel(cell_ref, recv_ref, out_ref, acc_ref):
    count, rows, pts = recv_ref.shape
    block = rows - EXTRA
    first = cell_ref[0]
    row_no = lax.broadcasted_iota(jnp.int32, (EXTRA, pts), 0)
    lane_no = lax.broadcasted_iota(jnp.int32, (EXTRA, pts), 1)
    coord_rows = (row_no % 4) != 3
    three_rows = row_no < 3

    def coords(extra):
        whole = jnp.where(coord_rows, extra + pltpu.roll(extra, 4, 0), 0.0)
        square = jnp.sum(jnp.where(three_rows, whole * whole, 0.0), axis=0, keepdims=True)
        return whole, square

    def rows_of(parts):
        high, mid, low = parts
        picked = jnp.where(row_no == 1, mid, low)
        return jnp.where(three_rows, jnp.where(row_no == 0, high, picked), 0.0)

    left = []
    masks = []
    for member in range(CELL):
        extra = recv_ref[first + member, block:rows, :].astype(F32)
        masks.append(extra[3:4, :])
        whole, square = coords(extra)
        parts = split_parts(2.0 * EXP2_COEF * whole)
        own = split_parts(EXP2_BASE - EXP2_COEF * square)
        unit = jnp.where(three_rows | (row_no == 3 + member), 1.0, 0.0)
        left.append(jnp.concatenate([*parts, rows_of(own), unit], axis=0))
    left = jnp.concatenate(left, axis=1).astype(BF16)
    ones = jnp.where(three_rows, 1.0, 0.0)
    acc_ref[...] = jnp.zeros_like(acc_ref)

    def step(tile, carry):
        extra = recv_ref[tile, block:rows, :].astype(F32)
        whole, square = coords(extra)
        tail = rows_of(split_parts(-EXP2_COEF * square))
        for member in range(CELL):
            chosen = jnp.where(lane_no[0:1] == tile, masks[member], 0.0)
            flag = jnp.sum(chosen, axis=1, keepdims=True)
            tail = jnp.where(row_no == 3 + member, (flag - 1.0) * OFF_BIAS, tail)
        right = jnp.concatenate([extra, extra, extra, ones, tail], axis=0).astype(BF16)
        value = jnp.exp2(dot_tn(right, left)).astype(BF16)
        acc_ref[...] += dot_nn(recv_ref[tile, 0:block, :], value)
        return carry

    lax.fori_loop(0, count, step, 0)
    for member in range(CELL):
        out_ref[member] = acc_ref[:, member * pts : (member + 1) * pts].astype(BF16)


def send_field(field, out_ref):
    turned = field.T.astype(BF16)
    out_ref[...] = turned.reshape(out_ref.shape)


def leaf_kernel(near_ref, right_ref, iterate_ref, inverse_ref, field_ref, out_ref):
    parts, block, pts = near_ref.shape
    near = near_ref[...].reshape(parts * block, pts).astype(F32).T
    resid = right_ref[...] - shift_value * iterate_ref[...].astype(F32) - near
    field = dot_nn(inverse_ref[0], resid.astype(BF16))
    field_ref[...] = field
    send_field(field, out_ref)


def pick_kernel(level_no, recv_ref, skeleton_ref, out_ref):
    tiles, cols, pts = recv_ref.shape
    index = skeleton_ref[level_no]
    count = index.shape[1]
    tile_of = index // pts
    inner = index - tile_of * pts
    row_no = lax.broadcasted_iota(jnp.int32, (pts, count), 0)
    chosen = jnp.where(row_no == inner, 1.0, 0.0).astype(BF16)
    lanes = dot_nn(recv_ref[...].reshape(tiles * cols, pts), chosen)
    total = jnp.zeros((cols, count), F32)
    for tile in range(tiles):
        total = total + jnp.where(tile_of == tile, lanes[tile * cols : (tile + 1) * cols], 0.0)
    total = total.astype(BF16)
    if len(out_ref.shape) == 2:
        out_ref[...] = total
    else:
        for copy in range(out_ref.shape[0]):
            out_ref[copy] = total


def solve_kernel(level_no, leaf_ref, nodes_ref, coupling_ref, inverse_ref, out_ref):
    half = nodes_ref.shape[0] // 2
    low = nodes_ref[0].astype(F32)
    high = nodes_ref[half].astype(F32)
    for member in range(1, half):
        low = low + nodes_ref[member].astype(F32)
        high = high + nodes_ref[half + member].astype(F32)
    upper = ((leaf_ref[0] >> level_no) & 1) == 1
    own = jnp.where(upper, high, low)
    other = jnp.where(upper, low, high)
    rhs = own - dot_nt(other.astype(BF16), coupling_ref[0, 0])
    answer = dot_nt(rhs.astype(BF16), inverse_ref[0, 0]).astype(BF16)
    for copy in range(out_ref.shape[0]):
        out_ref[copy] = answer


def lift_kernel(field_ref, lift_ref, answer_ref, *out_refs):
    tiles, cols, count = answer_ref.shape
    answer = answer_ref[...].reshape(tiles * cols, count)
    field = field_ref[...] - dot_nt(lift_ref[0], answer)
    out_refs[0][...] = field
    if len(out_refs) > 1:
        send_field(field, out_refs[1])


def level_spec(shape, level_no):
    tail = (0,) * (len(shape) - 1)
    return pl.BlockSpec((1,) + tuple(shape[1:]), lambda step: (level_no,) + tail)


def whole_spec(shape):
    zeros = (0,) * len(shape)
    return pl.BlockSpec(tuple(shape), lambda step: zeros)


def on_device(
    points, iterate, right_side, near_mask, leaf_inverse, skeleton, coupling, reduced_inverse, lift
):
    blk_count = lax.axis_size("blk")
    leaf_count = lax.axis_size("leaf")
    pts, cols = iterate.shape
    slots = skeleton.shape[2]
    share = cols // blk_count
    block = cols // CELL
    leaf_no = lax.axis_index("leaf").astype(jnp.int32).reshape(1)
    first = (lax.axis_index("blk") // CELL * CELL).astype(jnp.int32).reshape(1)
    cells = [list(range(c, c + CELL)) for c in range(0, blk_count, CELL)]

    packed = pl.pallas_call(
        pack_kernel,
        out_shape=jax.ShapeDtypeStruct((blk_count, block + EXTRA, pts), BF16),
        in_specs=[VMEM] * 3,
        out_specs=VMEM,
        scratch_shapes=[pltpu.VMEM((EXTRA, pts), F32)],
        name="pack",
    )(points, iterate, near_mask)
    packed = lax.all_to_all(packed, "blk", 0, 0)
    near = pl.pallas_call(
        near_kernel,
        out_shape=jax.ShapeDtypeStruct((CELL, block, pts), BF16),
        in_specs=[SMEM, VMEM],
        out_specs=VMEM,
        scratch_shapes=[pltpu.VMEM((block, CELL * pts), F32)],
        name="near",
    )(first, packed)
    near = lax.all_to_all(near, "blk", 0, 0, axis_index_groups=cells)
    field_shape = jax.ShapeDtypeStruct((pts, cols), F32)
    send_shape = jax.ShapeDtypeStruct((blk_count, share, pts), BF16)
    field, sent = pl.pallas_call(
        leaf_kernel,
        out_shape=(field_shape, send_shape),
        in_specs=[VMEM] * 4,
        out_specs=(VMEM, VMEM),
        name="leaf",
    )(near, right_side, iterate, leaf_inverse)

    for level_no in range(LEVELS):
        width = 2 << level_no
        groups = [list(range(c, c + width)) for c in range(0, leaf_count, width)]
        spread = level_no == 2
        sent = lax.all_to_all(sent, "blk", 0, 0)
        node_shape = (width, share, slots)
        nodes = pl.pallas_call(
            lambda *refs, level_no=level_no: pick_kernel(level_no, *refs),
            out_shape=jax.ShapeDtypeStruct(node_shape if spread else node_shape[1:], BF16),
            in_specs=[VMEM] * 2,
            out_specs=VMEM,
            name="pick",
        )(sent, skeleton)
        if spread:
            nodes = lax.all_to_all(nodes, "leaf", 0, 0, axis_index_groups=groups)
        else:
            nodes = lax.all_gather(nodes, "leaf", axis=0, axis_index_groups=groups)
        answer_shape = (blk_count, share, slots)
        answer = pl.pallas_call(
            lambda *refs, level_no=level_no: solve_kernel(level_no, *refs),
            out_shape=jax.ShapeDtypeStruct(answer_shape, BF16),
            grid=(1,),
            in_specs=[
                SMEM,
                whole_spec(node_shape),
                level_spec(coupling.shape, level_no),
                level_spec(reduced_inverse.shape, level_no),
            ],
            out_specs=whole_spec(answer_shape),
            name="solve",
        )(leaf_no, nodes, coupling, reduced_inverse)
        answer = lax.all_to_all(answer, "blk", 0, 0)
        last = level_no == LEVELS - 1
        results = pl.pallas_call(
            lift_kernel,
            out_shape=(field_shape,) if last else (field_shape, send_shape),
            grid=(1,),
            in_specs=[
                whole_spec(field.shape),
                level_spec(lift.shape, level_no),
                whole_spec(answer_shape),
            ],
            out_specs=tuple(
                whole_spec(s.shape) for s in ((field_shape,) if last else (field_shape, send_shape))
            ),
            name="lift",
        )(field, lift, answer)
        field = results[0]
        sent = None if last else results[1]
    return field


def solution(mesh):
    in_specs = (
        P(None, ("leaf", "blk")),
        P(("leaf", "blk"), None),
        P(("leaf", "blk"), None),
        P(("leaf", "blk"), None),
        P(("leaf", "blk"), None, None),
        P(None, "leaf", None),
        P(None, "leaf", None, None),
        P(None, "leaf", None, None),
        P(None, ("leaf", "blk"), None),
    )
    out_specs = P(("leaf", "blk"), None)
    return jax.shard_map(
        on_device, mesh=mesh, in_specs=in_specs, out_specs=out_specs, check_vma=False
    )
```

```python
import math

import jax
import jax.numpy as jnp
from jax import lax
from jax.experimental import pallas as pl
from jax.experimental.pallas import tpu as pltpu
from jax.sharding import PartitionSpec as P

LEVELS = 3
CELL = 4

kernel_scale = 0.125
spread_coef = 4.0
shift_value = 1.0

EXTRA = 8
OFF_BIAS = 30000.0
EXP2_COEF = spread_coef * math.log2(math.e)
EXP2_BASE = math.log2(kernel_scale)

F32 = jnp.float32
BF16 = jnp.bfloat16
VMEM = pl.BlockSpec(memory_space=pltpu.VMEM)
SMEM = pl.BlockSpec(memory_space=pltpu.SMEM)


def dot_nt(left, right):
    return lax.dot_general(left, right, (((1,), (1,)), ((), ())), preferred_element_type=F32)


def dot_tn(left, right):
    return lax.dot_general(left, right, (((0,), (0,)), ((), ())), preferred_element_type=F32)


def dot_nn(left, right):
    return jnp.dot(left, right, preferred_element_type=F32)


def split_parts(value):
    high = value.astype(BF16).astype(F32)
    rest = value - high
    mid = rest.astype(BF16).astype(F32)
    return high, mid, (rest - mid).astype(BF16).astype(F32)


def pack_kernel(points_ref, iterate_ref, mask_ref, out_ref, extra_ref):
    count, rows, pts = out_ref.shape
    block = rows - EXTRA
    point = points_ref[...]
    high = point.astype(BF16).astype(F32)
    extra_ref[...] = jnp.zeros_like(extra_ref)
    extra_ref[0:3, :] = high
    extra_ref[3:4, 0 : mask_ref.shape[1]] = mask_ref[...].astype(F32)
    extra_ref[4:7, :] = point - high
    turned = iterate_ref[...].astype(F32).T.astype(BF16)
    extra = extra_ref[...].astype(BF16)
    for dest in range(count):
        part = dest % CELL
        out_ref[dest, 0:block, :] = turned[part * block : (part + 1) * block]
        out_ref[dest, block:rows, :] = extra


def near_kernel(cell_ref, recv_ref, out_ref, acc_ref):
    count, rows, pts = recv_ref.shape
    block = rows - EXTRA
    first = cell_ref[0]
    row_no = lax.broadcasted_iota(jnp.int32, (EXTRA, pts), 0)
    lane_no = lax.broadcasted_iota(jnp.int32, (EXTRA, pts), 1)
    coord_rows = (row_no % 4) != 3
    three_rows = row_no < 3

    def coords(extra):
        whole = jnp.where(coord_rows, extra + pltpu.roll(extra, 4, 0), 0.0)
        square = jnp.sum(jnp.where(three_rows, whole * whole, 0.0), axis=0, keepdims=True)
        return whole, square

    def rows_of(parts):
        high, mid, low = parts
        picked = jnp.where(row_no == 1, mid, low)
        return jnp.where(three_rows, jnp.where(row_no == 0, high, picked), 0.0)

    left = []
    masks = []
    for member in range(CELL):
        extra = recv_ref[first + member, block:rows, :].astype(F32)
        masks.append(extra[3:4, :])
        whole, square = coords(extra)
        parts = split_parts(2.0 * EXP2_COEF * whole)
        own = split_parts(EXP2_BASE - EXP2_COEF * square)
        unit = jnp.where(three_rows | (row_no == 3 + member), 1.0, 0.0)
        left.append(jnp.concatenate([*parts, rows_of(own), unit], axis=0))
    left = jnp.concatenate(left, axis=1).astype(BF16)
    ones = jnp.where(three_rows, 1.0, 0.0)
    acc_ref[...] = jnp.zeros_like(acc_ref)

    def step(tile, carry):
        extra = recv_ref[tile, block:rows, :].astype(F32)
        whole, square = coords(extra)
        tail = rows_of(split_parts(-EXP2_COEF * square))
        for member in range(CELL):
            chosen = jnp.where(lane_no[0:1] == tile, masks[member], 0.0)
            flag = jnp.sum(chosen, axis=1, keepdims=True)
            tail = jnp.where(row_no == 3 + member, (flag - 1.0) * OFF_BIAS, tail)
        right = jnp.concatenate([extra, extra, extra, ones, tail], axis=0).astype(BF16)
        value = jnp.exp2(dot_tn(right, left)).astype(BF16)
        acc_ref[...] += dot_nn(recv_ref[tile, 0:block, :], value)
        return carry

    lax.fori_loop(0, count, step, 0)
    for member in range(CELL):
        out_ref[member] = acc_ref[:, member * pts : (member + 1) * pts].astype(BF16)


def send_field(field, out_ref):
    turned = field.T.astype(BF16)
    out_ref[...] = turned.reshape(out_ref.shape)


def leaf_kernel(near_ref, right_ref, iterate_ref, inverse_ref, field_ref, out_ref):
    parts, block, pts = near_ref.shape
    near = near_ref[...].reshape(parts * block, pts).astype(F32).T
    resid = right_ref[...] - shift_value * iterate_ref[...].astype(F32) - near
    field = dot_nn(inverse_ref[0], resid.astype(BF16))
    field_ref[...] = field
    send_field(field, out_ref)


def pick_rows(field, index):
    tiles, cols, pts = field.shape
    count = index.shape[1]
    tile_of = index // pts
    inner = index - tile_of * pts
    row_no = lax.broadcasted_iota(jnp.int32, (pts, count), 0)
    chosen = jnp.where(row_no == inner, 1.0, 0.0).astype(BF16)
    lanes = dot_nn(field.reshape(tiles * cols, pts), chosen)
    total = jnp.zeros((cols, count), F32)
    for tile in range(tiles):
        total = total + jnp.where(tile_of == tile, lanes[tile * cols : (tile + 1) * cols], 0.0)
    return total.astype(BF16)


def store_copies(value, out_ref):
    if len(out_ref.shape) == 2:
        out_ref[...] = value
    else:
        for copy in range(out_ref.shape[0]):
            out_ref[copy] = value


def pick_kernel(recv_ref, skeleton_ref, out_ref):
    store_copies(pick_rows(recv_ref[...], skeleton_ref[0]), out_ref)


def update_kernel(level_no, field_ref, answer_ref, lift_ref, skeleton_ref, next_ref, out_ref):
    step = pl.program_id(0)
    answer = answer_ref[...]
    tiles = lift_ref.shape[0]
    for tile in range(tiles):
        spot = step * tiles + tile
        next_ref[spot] = field_ref[spot].astype(F32) - dot_nt(answer, lift_ref[tile])

    @pl.when(step == pl.num_programs(0) - 1)
    def _():
        store_copies(pick_rows(next_ref[...].astype(BF16), skeleton_ref[level_no + 1]), out_ref)


def solve_kernel(level_no, leaf_ref, nodes_ref, coupling_ref, inverse_ref, *refs):
    half = nodes_ref.shape[0] // 2
    low = nodes_ref[0].astype(F32)
    high = nodes_ref[half].astype(F32)
    for member in range(1, half):
        low = low + nodes_ref[member].astype(F32)
        high = high + nodes_ref[half + member].astype(F32)
    upper = ((leaf_ref[0] >> level_no) & 1) == 1
    own = jnp.where(upper, high, low)
    other = jnp.where(upper, low, high)
    rhs = own - dot_nt(other.astype(BF16), coupling_ref[0, 0])
    answer = dot_nt(rhs.astype(BF16), inverse_ref[0, 0]).astype(BF16)
    share = answer.shape[0]
    earlier, out_ref = refs[:-1], refs[-1]
    for spot, value_ref in enumerate(earlier):
        out_ref[spot * share : (spot + 1) * share] = value_ref[...]
    out_ref[len(earlier) * share : (len(earlier) + 1) * share] = answer


def lift_kernel(field_ref, lift_ref, answer_ref, out_ref):
    blocks, rows, count = answer_ref.shape
    share = rows // LEVELS
    field = field_ref[...]
    for level_no in range(LEVELS):
        answer = answer_ref[:, level_no * share : (level_no + 1) * share, :]
        field = field - dot_nt(lift_ref[level_no], answer.reshape(blocks * share, count))
    out_ref[...] = field


def level_spec(shape, level_no):
    tail = (0,) * (len(shape) - 1)
    return pl.BlockSpec((1,) + tuple(shape[1:]), lambda step: (level_no,) + tail)


def whole_spec(shape):
    zeros = (0,) * len(shape)
    return pl.BlockSpec(tuple(shape), lambda step: zeros)


def on_device(
    points, iterate, right_side, near_mask, leaf_inverse, skeleton, coupling, reduced_inverse, lift
):
    blk_count = lax.axis_size("blk")
    leaf_count = lax.axis_size("leaf")
    pts, cols = iterate.shape
    slots = skeleton.shape[2]
    share = cols // blk_count
    block = cols // CELL
    leaf_no = lax.axis_index("leaf").astype(jnp.int32).reshape(1)
    first = (lax.axis_index("blk") // CELL * CELL).astype(jnp.int32).reshape(1)
    cells = [list(range(c, c + CELL)) for c in range(0, blk_count, CELL)]

    lifts = [lax.all_gather(lift[level_no], "blk", axis=0) for level_no in range(LEVELS - 1)]
    packed = pl.pallas_call(
        pack_kernel,
        out_shape=jax.ShapeDtypeStruct((blk_count, block + EXTRA, pts), BF16),
        in_specs=[VMEM] * 3,
        out_specs=VMEM,
        scratch_shapes=[pltpu.VMEM((EXTRA, pts), F32)],
        name="pack",
    )(points, iterate, near_mask)
    packed = lax.all_to_all(packed, "blk", 0, 0)
    near = pl.pallas_call(
        near_kernel,
        out_shape=jax.ShapeDtypeStruct((CELL, block, pts), BF16),
        in_specs=[SMEM, VMEM],
        out_specs=VMEM,
        scratch_shapes=[pltpu.VMEM((block, CELL * pts), F32)],
        name="near",
    )(first, packed)
    near = lax.all_to_all(near, "blk", 0, 0, axis_index_groups=cells)
    field_shape = jax.ShapeDtypeStruct((pts, cols), F32)
    send_shape = jax.ShapeDtypeStruct((blk_count, share, pts), BF16)
    field, sent = pl.pallas_call(
        leaf_kernel,
        out_shape=(field_shape, send_shape),
        in_specs=[VMEM] * 4,
        out_specs=(VMEM, VMEM),
        name="leaf",
    )(near, right_side, iterate, leaf_inverse)

    sent = lax.all_to_all(sent, "blk", 0, 0)
    answers = []
    for level_no in range(LEVELS):
        last = level_no == LEVELS - 1
        width = 2 << level_no
        groups = [list(range(c, c + width)) for c in range(0, leaf_count, width)]
        spread = level_no == 2
        node_shape = (width, share, slots)
        pick_shape = jax.ShapeDtypeStruct(node_shape if spread else node_shape[1:], BF16)
        if level_no == 0:
            nodes = pl.pallas_call(
                pick_kernel,
                out_shape=pick_shape,
                in_specs=[VMEM] * 2,
                out_specs=VMEM,
                name="pick",
            )(sent, skeleton)
        else:
            kept_shape = jax.ShapeDtypeStruct(sent.shape, F32)
            sent, nodes = pl.pallas_call(
                lambda *refs, level_no=level_no - 1: update_kernel(level_no, *refs),
                out_shape=(kept_shape, pick_shape),
                grid=(blk_count // CELL,),
                in_specs=[
                    whole_spec(sent.shape),
                    whole_spec((share, slots)),
                    pl.BlockSpec((CELL, pts, slots), lambda step: (step, 0, 0)),
                    whole_spec(skeleton.shape),
                ],
                out_specs=(whole_spec(kept_shape.shape), whole_spec(pick_shape.shape)),
                name="update",
            )(sent, answers[-1], lifts[level_no - 1], skeleton)
        if spread:
            nodes = lax.all_to_all(nodes, "leaf", 0, 0, axis_index_groups=groups)
        else:
            nodes = lax.all_gather(nodes, "leaf", axis=0, axis_index_groups=groups)
        earlier = answers if last else []
        answer_shape = ((len(earlier) + 1) * share, slots)
        answer = pl.pallas_call(
            lambda *refs, level_no=level_no: solve_kernel(level_no, *refs),
            out_shape=jax.ShapeDtypeStruct(answer_shape, BF16),
            grid=(1,),
            in_specs=[
                SMEM,
                whole_spec(node_shape),
                level_spec(coupling.shape, level_no),
                level_spec(reduced_inverse.shape, level_no),
            ]
            + [whole_spec((share, slots))] * len(earlier),
            out_specs=whole_spec(answer_shape),
            name="solve",
        )(leaf_no, nodes, coupling, reduced_inverse, *earlier)
        answers.append(answer)
    answer = lax.all_gather(answers[-1], "blk", axis=0)
    return pl.pallas_call(
        lift_kernel,
        out_shape=field_shape,
        in_specs=[VMEM] * 3,
        out_specs=VMEM,
        name="lift",
    )(field, lift, answer)


def solution(mesh):
    in_specs = (
        P(None, ("leaf", "blk")),
        P(("leaf", "blk"), None),
        P(("leaf", "blk"), None),
        P(("leaf", "blk"), None),
        P(("leaf", "blk"), None, None),
        P(None, "leaf", None),
        P(None, "leaf", None, None),
        P(None, "leaf", None, None),
        P(None, ("leaf", "blk"), None),
    )
    out_specs = P(("leaf", "blk"), None)
    return jax.shard_map(
        on_device, mesh=mesh, in_specs=in_specs, out_specs=out_specs, check_vma=False
    )
```

```python
import math

import jax
import jax.numpy as jnp
from jax import lax
from jax.experimental import pallas as pl
from jax.experimental.pallas import tpu as pltpu
from jax.sharding import PartitionSpec as P

LEVELS = 3
CELL = 4
ROOM = 64

kernel_scale = 0.125
spread_coef = 4.0
shift_value = 1.0

EXTRA = 8
OFF_BIAS = 30000.0
EXP2_COEF = spread_coef * math.log2(math.e)
EXP2_BASE = math.log2(kernel_scale)

F32 = jnp.float32
BF16 = jnp.bfloat16
VMEM = pl.BlockSpec(memory_space=pltpu.VMEM)
SMEM = pl.BlockSpec(memory_space=pltpu.SMEM)


def dot_nt(left, right):
    return lax.dot_general(left, right, (((1,), (1,)), ((), ())), preferred_element_type=F32)


def dot_tn(left, right):
    return lax.dot_general(left, right, (((0,), (0,)), ((), ())), preferred_element_type=F32)


def dot_nn(left, right):
    return jnp.dot(left, right, preferred_element_type=F32)


def split_parts(value):
    high = value.astype(BF16).astype(F32)
    rest = value - high
    mid = rest.astype(BF16).astype(F32)
    return high, mid, (rest - mid).astype(BF16).astype(F32)


def pack_kernel(points_ref, iterate_ref, mask_ref, out_ref, extra_ref):
    count, rows, pts = out_ref.shape
    block = rows - EXTRA
    point = points_ref[...]
    high = point.astype(BF16).astype(F32)
    extra_ref[...] = jnp.zeros_like(extra_ref)
    extra_ref[0:3, :] = high
    extra_ref[3:4, 0 : mask_ref.shape[1]] = mask_ref[...].astype(F32)
    extra_ref[4:7, :] = point - high
    turned = iterate_ref[...].astype(F32).T.astype(BF16)
    extra = extra_ref[...].astype(BF16)
    for dest in range(count):
        part = dest % CELL
        out_ref[dest, 0:block, :] = turned[part * block : (part + 1) * block]
        out_ref[dest, block:rows, :] = extra


def near_kernel(cell_ref, recv_ref, out_ref, acc_ref):
    count, rows, pts = recv_ref.shape
    block = rows - EXTRA
    first = cell_ref[0]
    row_no = lax.broadcasted_iota(jnp.int32, (EXTRA, pts), 0)
    lane_no = lax.broadcasted_iota(jnp.int32, (EXTRA, pts), 1)
    coord_rows = (row_no % 4) != 3
    three_rows = row_no < 3

    def coords(extra):
        whole = jnp.where(coord_rows, extra + pltpu.roll(extra, 4, 0), 0.0)
        square = jnp.sum(jnp.where(three_rows, whole * whole, 0.0), axis=0, keepdims=True)
        return whole, square

    def rows_of(parts):
        high, mid, low = parts
        picked = jnp.where(row_no == 1, mid, low)
        return jnp.where(three_rows, jnp.where(row_no == 0, high, picked), 0.0)

    left = []
    masks = []
    for member in range(CELL):
        extra = recv_ref[first + member, block:rows, :].astype(F32)
        masks.append(extra[3:4, :])
        whole, square = coords(extra)
        parts = split_parts(2.0 * EXP2_COEF * whole)
        own = split_parts(EXP2_BASE - EXP2_COEF * square)
        unit = jnp.where(three_rows | (row_no == 3 + member), 1.0, 0.0)
        left.append(jnp.concatenate([*parts, rows_of(own), unit], axis=0))
    left = jnp.concatenate(left, axis=1).astype(BF16)
    ones = jnp.where(three_rows, 1.0, 0.0)
    acc_ref[...] = jnp.zeros_like(acc_ref)

    def step(tile, carry):
        extra = recv_ref[tile, block:rows, :].astype(F32)
        whole, square = coords(extra)
        tail = rows_of(split_parts(-EXP2_COEF * square))
        for member in range(CELL):
            chosen = jnp.where(lane_no[0:1] == tile, masks[member], 0.0)
            flag = jnp.sum(chosen, axis=1, keepdims=True)
            tail = jnp.where(row_no == 3 + member, (flag - 1.0) * OFF_BIAS, tail)
        right = jnp.concatenate([extra, extra, extra, ones, tail], axis=0).astype(BF16)
        value = jnp.exp2(dot_tn(right, left)).astype(BF16)
        acc_ref[...] += dot_nn(recv_ref[tile, 0:block, :], value)
        return carry

    lax.fori_loop(0, count, step, 0)
    for member in range(CELL):
        out_ref[member] = acc_ref[:, member * pts : (member + 1) * pts].astype(BF16)


def send_field(field, out_ref):
    turned = field.T.astype(BF16)
    out_ref[...] = turned.reshape(out_ref.shape)


def leaf_kernel(near_ref, right_ref, iterate_ref, inverse_ref, field_ref, out_ref):
    parts, block, pts = near_ref.shape
    near = near_ref[...].reshape(parts * block, pts).astype(F32).T
    resid = right_ref[...] - shift_value * iterate_ref[...].astype(F32) - near
    field = dot_nn(inverse_ref[0], resid.astype(BF16))
    field_ref[...] = field
    send_field(field, out_ref)


def equal_rows(count, value, kind):
    row_no = lax.broadcasted_iota(jnp.int32, (count, value.shape[1]), 0)
    return jnp.where(row_no == value, 1.0, 0.0).astype(kind)


def pick_rows(field, index):
    tiles, cols, pts = field.shape
    tile_of = index // pts
    chosen = equal_rows(pts, index - tile_of * pts, BF16)
    lanes = dot_nn(field.reshape(tiles * cols, pts), chosen)
    total = jnp.zeros((cols, index.shape[1]), F32)
    for tile in range(tiles):
        total = total + jnp.where(tile_of == tile, lanes[tile * cols : (tile + 1) * cols], 0.0)
    return total


def store_copies(value, out_ref):
    if len(out_ref.shape) == 2:
        out_ref[...] = value
    else:
        for copy in range(out_ref.shape[0]):
            out_ref[copy] = value


def pick_kernel(recv_ref, skeleton_ref, *out_refs):
    for level_no in range(LEVELS):
        out_refs[level_no][...] = pick_rows(recv_ref[...], skeleton_ref[level_no]).astype(BF16)


def plan_kernel(tiles, tile_ref, skeleton_ref, lift_ref, rows_ref, slot_ref, over_ref):
    pts = lift_ref.shape[1]
    row_no = lax.broadcasted_iota(jnp.int32, (pts, pts), 0)
    lane_no = lax.broadcasted_iota(jnp.int32, (pts, pts), 1)
    before = jnp.where(row_no < lane_no, 1.0, 0.0).astype(BF16)
    own = lax.broadcasted_iota(jnp.int32, (tiles, pts), 0) == tile_ref[0]
    room_no = lax.broadcasted_iota(jnp.int32, (ROOM, pts), 0).astype(F32)
    most = jnp.zeros((tiles, pts), F32)
    spot = 0
    for level_no in range(1, LEVELS):
        index = skeleton_ref[level_no]
        tile_of = index // pts
        inner = equal_rows(pts, index - tile_of * pts, BF16)
        member = equal_rows(tiles, tile_of, F32)
        present = dot_nt(member.astype(BF16), inner)
        rank = dot_nn(present.astype(BF16), before)
        ranks = jnp.sum(member * dot_nn(rank.astype(BF16), inner), axis=0, keepdims=True)
        slot_ref[level_no - 1] = tile_of * ROOM + ranks.astype(jnp.int32)
        most = jnp.maximum(most, rank + present)
        own_present = jnp.sum(jnp.where(own, present, 0.0), axis=0, keepdims=True)
        own_rank = jnp.sum(jnp.where(own, rank, 0.0), axis=0, keepdims=True)
        chosen = jnp.where((room_no == own_rank) & (own_present > 0.5), 1.0, 0.0).astype(BF16)
        for earlier in range(level_no):
            rows_ref[spot * ROOM : (spot + 1) * ROOM] = dot_nn(chosen, lift_ref[earlier]).astype(BF16)
            spot += 1
    over_ref[0] = (jnp.max(most) > ROOM).astype(jnp.int32)


def fast_kernel(level_no, picked_ref, slot_ref, *refs):
    answer_refs, row_refs, out_ref = refs[:level_no], refs[level_no:-1], refs[-1]
    tiles, room, count = row_refs[0].shape
    total = jnp.zeros((answer_refs[0].shape[0], tiles * room), F32)
    for answer_ref, row_ref in zip(answer_refs, row_refs):
        total = total + dot_nt(answer_ref[...], row_ref[...].reshape(tiles * room, count))
    high = total.astype(BF16)
    low = (total - high.astype(F32)).astype(BF16)
    chosen = equal_rows(tiles * room, slot_ref[level_no - 1], BF16)
    change = dot_nn(high, chosen) + dot_nn(low, chosen)
    store_copies((picked_ref[...].astype(F32) - change).astype(BF16), out_ref)


def copy_kernel(*refs):
    share = refs[0].shape[0]
    for spot, value_ref in enumerate(refs[:-1]):
        for copy in range(refs[-1].shape[0]):
            refs[-1][copy, spot * share : (spot + 1) * share, :] = value_ref[...]


def tile_kernel(lift_ref, answer_ref, out_ref):
    blocks, rows, count = answer_ref.shape
    share = out_ref.shape[1]
    total = jnp.zeros((lift_ref.shape[1], blocks * share), F32)
    for earlier in range(rows // share):
        answer = answer_ref[:, earlier * share : (earlier + 1) * share, :]
        total = total + dot_nt(lift_ref[earlier], answer.reshape(blocks * share, count))
    send_field(total, out_ref)


def less_kernel(level_no, picked_ref, recv_ref, skeleton_ref, out_ref):
    change = pick_rows(recv_ref[...], skeleton_ref[level_no])
    store_copies((picked_ref[...].astype(F32) - change).astype(BF16), out_ref)


def solve_kernel(level_no, leaf_ref, nodes_ref, coupling_ref, inverse_ref, *refs):
    half = nodes_ref.shape[0] // 2
    low = nodes_ref[0].astype(F32)
    high = nodes_ref[half].astype(F32)
    for member in range(1, half):
        low = low + nodes_ref[member].astype(F32)
        high = high + nodes_ref[half + member].astype(F32)
    upper = ((leaf_ref[0] >> level_no) & 1) == 1
    own = jnp.where(upper, high, low)
    other = jnp.where(upper, low, high)
    rhs = own - dot_nt(other.astype(BF16), coupling_ref[0, 0])
    answer = dot_nt(rhs.astype(BF16), inverse_ref[0, 0]).astype(BF16)
    share = answer.shape[0]
    earlier, out_ref = refs[:-1], refs[-1]
    for spot, value_ref in enumerate(earlier):
        out_ref[spot * share : (spot + 1) * share] = value_ref[...]
    out_ref[len(earlier) * share : (len(earlier) + 1) * share] = answer


def lift_kernel(field_ref, lift_ref, answer_ref, out_ref):
    blocks, rows, count = answer_ref.shape
    share = rows // LEVELS
    field = field_ref[...]
    for level_no in range(LEVELS):
        answer = answer_ref[:, level_no * share : (level_no + 1) * share, :]
        field = field - dot_nt(lift_ref[level_no], answer.reshape(blocks * share, count))
    out_ref[...] = field


def level_spec(shape, level_no):
    tail = (0,) * (len(shape) - 1)
    return pl.BlockSpec((1,) + tuple(shape[1:]), lambda step: (level_no,) + tail)


def whole_spec(shape):
    zeros = (0,) * len(shape)
    return pl.BlockSpec(tuple(shape), lambda step: zeros)


def on_device(
    points, iterate, right_side, near_mask, leaf_inverse, skeleton, coupling, reduced_inverse, lift
):
    blk_count = lax.axis_size("blk")
    leaf_count = lax.axis_size("leaf")
    pts, cols = iterate.shape
    slots = skeleton.shape[2]
    share = cols // blk_count
    block = cols // CELL
    leaf_no = lax.axis_index("leaf").astype(jnp.int32).reshape(1)
    first = (lax.axis_index("blk") // CELL * CELL).astype(jnp.int32).reshape(1)
    cells = [list(range(c, c + CELL)) for c in range(0, blk_count, CELL)]

    tile_no = lax.axis_index("blk").astype(jnp.int32).reshape(1)
    pairs = LEVELS * (LEVELS - 1) // 2
    rows, slot_of, over = pl.pallas_call(
        lambda *refs: plan_kernel(blk_count, *refs),
        out_shape=(
            jax.ShapeDtypeStruct((pairs * ROOM, slots), BF16),
            jax.ShapeDtypeStruct((LEVELS - 1, 1, slots), jnp.int32),
            jax.ShapeDtypeStruct((1,), jnp.int32),
        ),
        in_specs=[SMEM, VMEM, VMEM],
        out_specs=(VMEM, VMEM, SMEM),
        name="plan",
    )(tile_no, skeleton, lift)
    rows = lax.all_gather(rows, "blk", axis=0)
    packed = pl.pallas_call(
        pack_kernel,
        out_shape=jax.ShapeDtypeStruct((blk_count, block + EXTRA, pts), BF16),
        in_specs=[VMEM] * 3,
        out_specs=VMEM,
        scratch_shapes=[pltpu.VMEM((EXTRA, pts), F32)],
        name="pack",
    )(points, iterate, near_mask)
    packed = lax.all_to_all(packed, "blk", 0, 0)
    near = pl.pallas_call(
        near_kernel,
        out_shape=jax.ShapeDtypeStruct((CELL, block, pts), BF16),
        in_specs=[SMEM, VMEM],
        out_specs=VMEM,
        scratch_shapes=[pltpu.VMEM((block, CELL * pts), F32)],
        name="near",
    )(first, packed)
    near = lax.all_to_all(near, "blk", 0, 0, axis_index_groups=cells)
    field_shape = jax.ShapeDtypeStruct((pts, cols), F32)
    send_shape = jax.ShapeDtypeStruct((blk_count, share, pts), BF16)
    field, sent = pl.pallas_call(
        leaf_kernel,
        out_shape=(field_shape, send_shape),
        in_specs=[VMEM] * 4,
        out_specs=(VMEM, VMEM),
        name="leaf",
    )(near, right_side, iterate, leaf_inverse)

    sent = lax.all_to_all(sent, "blk", 0, 0)
    small_shape = jax.ShapeDtypeStruct((share, slots), BF16)
    picked = pl.pallas_call(
        pick_kernel,
        out_shape=(small_shape,) * LEVELS,
        in_specs=[VMEM] * 2,
        out_specs=(VMEM,) * LEVELS,
        name="pick",
    )(sent, skeleton)

    def fast(level_no, shape, answers):
        offset = level_no * (level_no - 1) // 2
        return pl.pallas_call(
            lambda *refs: fast_kernel(level_no, *refs),
            out_shape=shape,
            grid=(1,),
            in_specs=[whole_spec((share, slots)), whole_spec(slot_of.shape)]
            + [whole_spec((share, slots))] * level_no
            + [
                pl.BlockSpec((blk_count, ROOM, slots), lambda step, spot=offset + k: (0, spot, 0))
                for k in range(level_no)
            ],
            out_specs=whole_spec(shape.shape),
            name="fast",
        )(picked[level_no], slot_of, *answers, *[rows] * level_no)

    def slow(level_no, shape, answers):
        copies = pl.pallas_call(
            copy_kernel,
            out_shape=jax.ShapeDtypeStruct((blk_count, level_no * share, slots), BF16),
            in_specs=[VMEM] * level_no,
            out_specs=VMEM,
            name="copies",
        )(*answers)
        copies = lax.all_to_all(copies, "blk", 0, 0)
        change = pl.pallas_call(
            tile_kernel,
            out_shape=send_shape,
            in_specs=[VMEM] * 2,
            out_specs=VMEM,
            name="tile",
        )(lift, copies)
        change = lax.all_to_all(change, "blk", 0, 0)
        return pl.pallas_call(
            lambda *refs: less_kernel(level_no, *refs),
            out_shape=shape,
            in_specs=[VMEM] * 3,
            out_specs=VMEM,
            name="less",
        )(picked[level_no], change, skeleton)

    answers = []
    for level_no in range(LEVELS):
        last = level_no == LEVELS - 1
        width = 2 << level_no
        groups = [list(range(c, c + width)) for c in range(0, leaf_count, width)]
        spread = level_no == 2
        node_shape = (width, share, slots)
        if level_no == 0:
            nodes = picked[0]
        else:
            pick_shape = jax.ShapeDtypeStruct(node_shape if spread else node_shape[1:], BF16)
            nodes = lax.cond(
                over[0] > 0,
                lambda *given, level_no=level_no: slow(level_no, pick_shape, given),
                lambda *given, level_no=level_no: fast(level_no, pick_shape, given),
                *answers,
            )
        if spread:
            nodes = lax.all_to_all(nodes, "leaf", 0, 0, axis_index_groups=groups)
        else:
            nodes = lax.all_gather(nodes, "leaf", axis=0, axis_index_groups=groups)
        earlier = answers if last else []
        answer_shape = ((len(earlier) + 1) * share, slots)
        answer = pl.pallas_call(
            lambda *refs, level_no=level_no: solve_kernel(level_no, *refs),
            out_shape=jax.ShapeDtypeStruct(answer_shape, BF16),
            grid=(1,),
            in_specs=[
                SMEM,
                whole_spec(node_shape),
                level_spec(coupling.shape, level_no),
                level_spec(reduced_inverse.shape, level_no),
            ]
            + [whole_spec((share, slots))] * len(earlier),
            out_specs=whole_spec(answer_shape),
            name="solve",
        )(leaf_no, nodes, coupling, reduced_inverse, *earlier)
        answers.append(answer)
    answer = lax.all_gather(answers[-1], "blk", axis=0)
    return pl.pallas_call(
        lift_kernel,
        out_shape=field_shape,
        in_specs=[VMEM] * 3,
        out_specs=VMEM,
        name="lift",
    )(field, lift, answer)


def solution(mesh):
    in_specs = (
        P(None, ("leaf", "blk")),
        P(("leaf", "blk"), None),
        P(("leaf", "blk"), None),
        P(("leaf", "blk"), None),
        P(("leaf", "blk"), None, None),
        P(None, "leaf", None),
        P(None, "leaf", None, None),
        P(None, "leaf", None, None),
        P(None, ("leaf", "blk"), None),
    )
    out_specs = P(("leaf", "blk"), None)
    return jax.shard_map(
        on_device, mesh=mesh, in_specs=in_specs, out_specs=out_specs, check_vma=False
    )
```

```python
import math

import jax
import jax.numpy as jnp
from jax import lax
from jax.experimental import pallas as pl
from jax.experimental.pallas import tpu as pltpu
from jax.sharding import PartitionSpec as P

LEVELS = 3
CELL = 8
CHUNK = 1024
ROOM = 64
KERNEL_BYTES = 16 << 20

kernel_scale = 0.125
spread_coef = 4.0
shift_value = 1.0

EXTRA = 8
OFF_BIAS = 30000.0
EXP2_COEF = spread_coef * math.log2(math.e)
EXP2_BASE = math.log2(kernel_scale)

F32 = jnp.float32
BF16 = jnp.bfloat16
PARAMS = pltpu.CompilerParams(vmem_limit_bytes=KERNEL_BYTES)
VMEM = pl.BlockSpec(memory_space=pltpu.VMEM)
SMEM = pl.BlockSpec(memory_space=pltpu.SMEM)


def dot_nt(left, right):
    return lax.dot_general(left, right, (((1,), (1,)), ((), ())), preferred_element_type=F32)


def dot_tn(left, right):
    return lax.dot_general(left, right, (((0,), (0,)), ((), ())), preferred_element_type=F32)


def dot_nn(left, right):
    return jnp.dot(left, right, preferred_element_type=F32)


def split_parts(value):
    high = value.astype(BF16).astype(F32)
    rest = value - high
    mid = rest.astype(BF16).astype(F32)
    return high, mid, (rest - mid).astype(BF16).astype(F32)


def pack_kernel(points_ref, iterate_ref, mask_ref, out_ref, extra_ref):
    count, rows, pts = out_ref.shape
    block = rows - EXTRA
    point = points_ref[...]
    high = point.astype(BF16).astype(F32)
    extra_ref[...] = jnp.zeros_like(extra_ref)
    extra_ref[0:3, :] = high
    extra_ref[3:4, 0 : mask_ref.shape[1]] = mask_ref[...].astype(F32)
    extra_ref[4:7, :] = point - high
    turned = iterate_ref[...].astype(F32).T.astype(BF16)
    extra = extra_ref[...].astype(BF16)
    for dest in range(count):
        part = dest % CELL
        out_ref[dest, 0:block, :] = turned[part * block : (part + 1) * block]
        out_ref[dest, block:rows, :] = extra


def near_kernel(cell_ref, recv_ref, out_ref, acc_ref, left_ref):
    count, rows, pts = recv_ref.shape
    block = rows - EXTRA
    first = cell_ref[0]
    row_no = lax.broadcasted_iota(jnp.int32, (EXTRA, pts), 0)
    coord_rows = (row_no % 4) != 3
    three_rows = row_no < 3
    ones = jnp.where(three_rows, 1.0, 0.0)

    def coords(extra):
        whole = jnp.where(coord_rows, extra + pltpu.roll(extra, 4, 0), 0.0)
        square = jnp.sum(jnp.where(three_rows, whole * whole, 0.0), axis=0, keepdims=True)
        return whole, square

    def rows_of(parts):
        high, mid, low = parts
        picked = jnp.where(row_no == 1, mid, low)
        return jnp.where(three_rows, jnp.where(row_no == 0, high, picked), 0.0)

    left = []
    cell_rows = lax.broadcasted_iota(jnp.int32, (CELL, pts), 0)
    tile_no = lax.broadcasted_iota(jnp.int32, (CELL, pts), 1)
    masks = jnp.zeros((CELL, pts), F32)
    for member in range(CELL):
        extra = recv_ref[first + member, block:rows, :].astype(F32)
        masks = jnp.where(cell_rows == member, extra[3:4, :], masks)
        whole, square = coords(extra)
        parts = split_parts(2.0 * EXP2_COEF * whole)
        own = split_parts(EXP2_BASE - EXP2_COEF * square)
        unit = jnp.where(cell_rows == member, 1.0, 0.0)
        value = jnp.concatenate([*parts, rows_of(own), ones, unit], axis=0).astype(BF16)
        left_ref[:, member * pts : (member + 1) * pts] = value
    acc_ref[...] = jnp.zeros_like(acc_ref)

    def step(tile, carry):
        extra = recv_ref[tile, block:rows, :].astype(F32)
        whole, square = coords(extra)
        tail = rows_of(split_parts(-EXP2_COEF * square))
        flag = jnp.sum(jnp.where(tile_no == tile, masks, 0.0), axis=1, keepdims=True)
        bias = jnp.broadcast_to((flag - 1.0) * OFF_BIAS, masks.shape)
        right = jnp.concatenate([extra, extra, extra, ones, tail, bias], axis=0).astype(BF16)
        iterate = recv_ref[tile, 0:block, :]
        for low in range(0, CELL * pts, CHUNK):
            span = slice(low, low + CHUNK)
            value = jnp.exp2(dot_tn(right, left_ref[:, span])).astype(BF16)
            acc_ref[:, span] += dot_nn(iterate, value)
        return carry

    lax.fori_loop(0, count, step, 0, unroll=2)
    for member in range(CELL):
        out_ref[member] = acc_ref[:, member * pts : (member + 1) * pts].astype(BF16)


def send_field(field, out_ref):
    turned = field.T.astype(BF16)
    out_ref[...] = turned.reshape(out_ref.shape)


def leaf_kernel(near_ref, right_ref, iterate_ref, inverse_ref, field_ref, out_ref):
    parts, block, pts = near_ref.shape
    near = near_ref[...].reshape(parts * block, pts).astype(F32).T
    resid = right_ref[...] - shift_value * iterate_ref[...].astype(F32) - near
    field = dot_nn(inverse_ref[0], resid.astype(BF16))
    field_ref[...] = field
    send_field(field, out_ref)


def equal_rows(count, value, kind):
    row_no = lax.broadcasted_iota(jnp.int32, (count, value.shape[1]), 0)
    return jnp.where(row_no == value, 1.0, 0.0).astype(kind)


def pick_rows(field, index):
    tiles, cols, pts = field.shape
    tile_of = index // pts
    chosen = equal_rows(pts, index - tile_of * pts, BF16)
    lanes = dot_nn(field.reshape(tiles * cols, pts), chosen)
    total = jnp.zeros((cols, index.shape[1]), F32)
    for tile in range(tiles):
        total = total + jnp.where(tile_of == tile, lanes[tile * cols : (tile + 1) * cols], 0.0)
    return total


def store_copies(value, out_ref):
    if len(out_ref.shape) == 2:
        out_ref[...] = value
    else:
        for copy in range(out_ref.shape[0]):
            out_ref[copy] = value


def pick_kernel(recv_ref, skeleton_ref, *out_refs):
    for level_no in range(LEVELS):
        out_refs[level_no][...] = pick_rows(recv_ref[...], skeleton_ref[level_no]).astype(BF16)


def plan_kernel(tiles, tile_ref, skeleton_ref, lift_ref, rows_ref, slot_ref, over_ref):
    pts = lift_ref.shape[1]
    row_no = lax.broadcasted_iota(jnp.int32, (pts, pts), 0)
    lane_no = lax.broadcasted_iota(jnp.int32, (pts, pts), 1)
    before = jnp.where(row_no < lane_no, 1.0, 0.0).astype(BF16)
    own = lax.broadcasted_iota(jnp.int32, (tiles, pts), 0) == tile_ref[0]
    room_no = lax.broadcasted_iota(jnp.int32, (ROOM, pts), 0).astype(F32)
    most = jnp.zeros((tiles, pts), F32)
    spot = 0
    for level_no in range(1, LEVELS):
        index = skeleton_ref[level_no]
        tile_of = index // pts
        inner = equal_rows(pts, index - tile_of * pts, BF16)
        member = equal_rows(tiles, tile_of, F32)
        present = dot_nt(member.astype(BF16), inner)
        rank = dot_nn(present.astype(BF16), before)
        ranks = jnp.sum(member * dot_nn(rank.astype(BF16), inner), axis=0, keepdims=True)
        slot_ref[level_no - 1] = tile_of * ROOM + ranks.astype(jnp.int32)
        most = jnp.maximum(most, rank + present)
        own_present = jnp.sum(jnp.where(own, present, 0.0), axis=0, keepdims=True)
        own_rank = jnp.sum(jnp.where(own, rank, 0.0), axis=0, keepdims=True)
        chosen = jnp.where((room_no == own_rank) & (own_present > 0.5), 1.0, 0.0).astype(BF16)
        for earlier in range(level_no):
            rows_ref[spot * ROOM : (spot + 1) * ROOM] = dot_nn(chosen, lift_ref[earlier]).astype(BF16)
            spot += 1
    over_ref[0] = (jnp.max(most) > ROOM).astype(jnp.int32)


def fast_kernel(level_no, picked_ref, slot_ref, *refs):
    answer_refs, row_refs, out_ref = refs[:level_no], refs[level_no:-1], refs[-1]
    tiles, room, count = row_refs[0].shape
    total = jnp.zeros((answer_refs[0].shape[0], tiles * room), F32)
    for answer_ref, row_ref in zip(answer_refs, row_refs):
        total = total + dot_nt(answer_ref[...], row_ref[...].reshape(tiles * room, count))
    high = total.astype(BF16)
    low = (total - high.astype(F32)).astype(BF16)
    chosen = equal_rows(tiles * room, slot_ref[level_no - 1], BF16)
    change = dot_nn(high, chosen) + dot_nn(low, chosen)
    store_copies((picked_ref[...].astype(F32) - change).astype(BF16), out_ref)


def copy_kernel(*refs):
    share = refs[0].shape[0]
    for spot, value_ref in enumerate(refs[:-1]):
        for copy in range(refs[-1].shape[0]):
            refs[-1][copy, spot * share : (spot + 1) * share, :] = value_ref[...]


def tile_kernel(lift_ref, answer_ref, out_ref):
    blocks, rows, count = answer_ref.shape
    share = out_ref.shape[1]
    total = jnp.zeros((lift_ref.shape[1], blocks * share), F32)
    for earlier in range(rows // share):
        answer = answer_ref[:, earlier * share : (earlier + 1) * share, :]
        total = total + dot_nt(lift_ref[earlier], answer.reshape(blocks * share, count))
    send_field(total, out_ref)


def less_kernel(level_no, picked_ref, recv_ref, skeleton_ref, out_ref):
    change = pick_rows(recv_ref[...], skeleton_ref[level_no])
    store_copies((picked_ref[...].astype(F32) - change).astype(BF16), out_ref)


def solve_kernel(level_no, leaf_ref, nodes_ref, coupling_ref, inverse_ref, *refs):
    half = nodes_ref.shape[0] // 2
    low = nodes_ref[0].astype(F32)
    high = nodes_ref[half].astype(F32)
    for member in range(1, half):
        low = low + nodes_ref[member].astype(F32)
        high = high + nodes_ref[half + member].astype(F32)
    upper = ((leaf_ref[0] >> level_no) & 1) == 1
    own = jnp.where(upper, high, low)
    other = jnp.where(upper, low, high)
    rhs = own - dot_nt(other.astype(BF16), coupling_ref[0, 0])
    answer = dot_nt(rhs.astype(BF16), inverse_ref[0, 0]).astype(BF16)
    share = answer.shape[0]
    earlier, out_ref = refs[:-1], refs[-1]
    for spot, value_ref in enumerate(earlier):
        out_ref[spot * share : (spot + 1) * share] = value_ref[...]
    out_ref[len(earlier) * share : (len(earlier) + 1) * share] = answer


def lift_kernel(field_ref, lift_ref, answer_ref, out_ref):
    blocks, rows, count = answer_ref.shape
    share = rows // LEVELS
    field = field_ref[...]
    for level_no in range(LEVELS):
        answer = answer_ref[:, level_no * share : (level_no + 1) * share, :]
        field = field - dot_nt(lift_ref[level_no], answer.reshape(blocks * share, count))
    out_ref[...] = field


def level_spec(shape, level_no):
    tail = (0,) * (len(shape) - 1)
    return pl.BlockSpec((1,) + tuple(shape[1:]), lambda step: (level_no,) + tail)


def whole_spec(shape):
    zeros = (0,) * len(shape)
    return pl.BlockSpec(tuple(shape), lambda step: zeros)


def on_device(
    points, iterate, right_side, near_mask, leaf_inverse, skeleton, coupling, reduced_inverse, lift
):
    blk_count = lax.axis_size("blk")
    leaf_count = lax.axis_size("leaf")
    pts, cols = iterate.shape
    slots = skeleton.shape[2]
    share = cols // blk_count
    block = cols // CELL
    leaf_no = lax.axis_index("leaf").astype(jnp.int32).reshape(1)
    first = (lax.axis_index("blk") // CELL * CELL).astype(jnp.int32).reshape(1)
    tile_no = lax.axis_index("blk").astype(jnp.int32).reshape(1)
    cells = [list(range(c, c + CELL)) for c in range(0, blk_count, CELL)]
    leaf_no, first, tile_no, points, skeleton = lax.optimization_barrier(
        (leaf_no, first, tile_no, points, skeleton)
    )

    pairs = LEVELS * (LEVELS - 1) // 2
    rows, slot_of, over = pl.pallas_call(
        lambda *refs: plan_kernel(blk_count, *refs),
        out_shape=(
            jax.ShapeDtypeStruct((pairs * ROOM, slots), BF16),
            jax.ShapeDtypeStruct((LEVELS - 1, 1, slots), jnp.int32),
            jax.ShapeDtypeStruct((1,), jnp.int32),
        ),
        in_specs=[SMEM, VMEM, VMEM],
        out_specs=(VMEM, VMEM, SMEM),
        compiler_params=PARAMS,
        name="plan",
    )(tile_no, skeleton, lift)
    rows = lax.all_gather(rows, "blk", axis=0)
    packed = pl.pallas_call(
        pack_kernel,
        out_shape=jax.ShapeDtypeStruct((blk_count, block + EXTRA, pts), BF16),
        in_specs=[VMEM] * 3,
        out_specs=VMEM,
        scratch_shapes=[pltpu.VMEM((EXTRA, pts), F32)],
        compiler_params=PARAMS,
        name="pack",
    )(points, iterate, near_mask)
    packed = lax.all_to_all(packed, "blk", 0, 0)
    near = pl.pallas_call(
        near_kernel,
        out_shape=jax.ShapeDtypeStruct((CELL, block, pts), BF16),
        in_specs=[SMEM, VMEM],
        out_specs=VMEM,
        scratch_shapes=[
            pltpu.VMEM((block, CELL * pts), F32),
            pltpu.VMEM((5 * EXTRA + CELL, CELL * pts), BF16),
        ],
        compiler_params=PARAMS,
        name="near",
    )(first, packed)
    near = lax.all_to_all(near, "blk", 0, 0, axis_index_groups=cells)
    field_shape = jax.ShapeDtypeStruct((pts, cols), F32)
    send_shape = jax.ShapeDtypeStruct((blk_count, share, pts), BF16)
    field, sent = pl.pallas_call(
        leaf_kernel,
        out_shape=(field_shape, send_shape),
        in_specs=[VMEM] * 4,
        out_specs=(VMEM, VMEM),
        compiler_params=PARAMS,
        name="leaf",
    )(near, right_side, iterate, leaf_inverse)

    sent = lax.all_to_all(sent, "blk", 0, 0)
    sent, over = lax.optimization_barrier((sent, over))
    small_shape = jax.ShapeDtypeStruct((share, slots), BF16)
    picked = pl.pallas_call(
        pick_kernel,
        out_shape=(small_shape,) * LEVELS,
        in_specs=[VMEM] * 2,
        out_specs=(VMEM,) * LEVELS,
        compiler_params=PARAMS,
        name="pick",
    )(sent, skeleton)

    def fast(level_no, shape, answers):
        offset = level_no * (level_no - 1) // 2
        return pl.pallas_call(
            lambda *refs: fast_kernel(level_no, *refs),
            out_shape=shape,
            grid=(1,),
            in_specs=[whole_spec((share, slots)), whole_spec(slot_of.shape)]
            + [whole_spec((share, slots))] * level_no
            + [
                pl.BlockSpec((blk_count, ROOM, slots), lambda step, spot=offset + k: (0, spot, 0))
                for k in range(level_no)
            ],
            out_specs=whole_spec(shape.shape),
            compiler_params=PARAMS,
            name="fast",
        )(picked[level_no], slot_of, *answers, *[rows] * level_no)

    def slow(level_no, shape, answers):
        copies = pl.pallas_call(
            copy_kernel,
            out_shape=jax.ShapeDtypeStruct((blk_count, level_no * share, slots), BF16),
            in_specs=[VMEM] * level_no,
            out_specs=VMEM,
            compiler_params=PARAMS,
            name="copies",
        )(*answers)
        copies = lax.all_to_all(copies, "blk", 0, 0)
        change = pl.pallas_call(
            tile_kernel,
            out_shape=send_shape,
            in_specs=[VMEM] * 2,
            out_specs=VMEM,
            compiler_params=PARAMS,
            name="tile",
        )(lift, copies)
        change = lax.all_to_all(change, "blk", 0, 0)
        return pl.pallas_call(
            lambda *refs: less_kernel(level_no, *refs),
            out_shape=shape,
            in_specs=[VMEM] * 3,
            out_specs=VMEM,
            compiler_params=PARAMS,
            name="less",
        )(picked[level_no], change, skeleton)

    answers = []
    for level_no in range(LEVELS):
        last = level_no == LEVELS - 1
        width = 2 << level_no
        groups = [list(range(c, c + width)) for c in range(0, leaf_count, width)]
        spread = level_no == 2
        node_shape = (width, share, slots)
        if level_no == 0:
            nodes = picked[0]
        else:
            pick_shape = jax.ShapeDtypeStruct(node_shape if spread else node_shape[1:], BF16)
            nodes = lax.cond(
                over[0] > 0,
                lambda *given, level_no=level_no: slow(level_no, pick_shape, given),
                lambda *given, level_no=level_no: fast(level_no, pick_shape, given),
                *answers,
            )
        if spread:
            nodes = lax.all_to_all(nodes, "leaf", 0, 0, axis_index_groups=groups)
        else:
            nodes = lax.all_gather(nodes, "leaf", axis=0, axis_index_groups=groups)
        earlier = answers if last else []
        answer_shape = ((len(earlier) + 1) * share, slots)
        answer = pl.pallas_call(
            lambda *refs, level_no=level_no: solve_kernel(level_no, *refs),
            out_shape=jax.ShapeDtypeStruct(answer_shape, BF16),
            grid=(1,),
            in_specs=[
                SMEM,
                whole_spec(node_shape),
                level_spec(coupling.shape, level_no),
                level_spec(reduced_inverse.shape, level_no),
            ]
            + [whole_spec((share, slots))] * len(earlier),
            out_specs=whole_spec(answer_shape),
            compiler_params=PARAMS,
            name="solve",
        )(leaf_no, nodes, coupling, reduced_inverse, *earlier)
        answers.append(answer)
    answer = lax.all_gather(answers[-1], "blk", axis=0)
    return pl.pallas_call(
        lift_kernel,
        out_shape=field_shape,
        in_specs=[VMEM] * 3,
        out_specs=VMEM,
        compiler_params=PARAMS,
        name="lift",
    )(field, lift, answer)


def solution(mesh):
    in_specs = (
        P(None, ("leaf", "blk")),
        P(("leaf", "blk"), None),
        P(("leaf", "blk"), None),
        P(("leaf", "blk"), None),
        P(("leaf", "blk"), None, None),
        P(None, "leaf", None),
        P(None, "leaf", None, None),
        P(None, "leaf", None, None),
        P(None, ("leaf", "blk"), None),
    )
    out_specs = P(("leaf", "blk"), None)
    return jax.shard_map(
        on_device, mesh=mesh, in_specs=in_specs, out_specs=out_specs, check_vma=False
    )
```

```python
import math

import jax
import jax.numpy as jnp
from jax import lax
from jax.experimental import pallas as pl
from jax.experimental.pallas import tpu as pltpu
from jax.sharding import PartitionSpec as P

LEVELS = 3
CELL = 8
CHUNK = 2048
ROOM = 64
KERNEL_BYTES = 16 << 20

kernel_scale = 0.125
spread_coef = 4.0
shift_value = 1.0

EXTRA = 8
OFF_BIAS = 30000.0
EXP2_COEF = spread_coef * math.log2(math.e)
EXP2_BASE = math.log2(kernel_scale)

F32 = jnp.float32
BF16 = jnp.bfloat16
PARAMS = pltpu.CompilerParams(vmem_limit_bytes=KERNEL_BYTES)
VMEM = pl.BlockSpec(memory_space=pltpu.VMEM)
SMEM = pl.BlockSpec(memory_space=pltpu.SMEM)
ANY = pl.BlockSpec(memory_space=pl.ANY)


def dot_nt(left, right):
    return lax.dot_general(left, right, (((1,), (1,)), ((), ())), preferred_element_type=F32)


def dot_tn(left, right):
    return lax.dot_general(left, right, (((0,), (0,)), ((), ())), preferred_element_type=F32)


def dot_nn(left, right):
    return jnp.dot(left, right, preferred_element_type=F32)


def split_parts(value):
    high = value.astype(BF16).astype(F32)
    rest = value - high
    mid = rest.astype(BF16).astype(F32)
    return high, mid, (rest - mid).astype(BF16).astype(F32)


def pack_kernel(*refs):
    sources, out_ref, extra_ref = refs[:3], refs[3], refs[4]
    points_ref, iterate_ref, mask_ref = refs[5:8]
    copies = [
        pltpu.make_async_copy(source, target, refs[8].at[spot])
        for spot, (source, target) in enumerate(zip(sources, refs[5:8]))
    ]
    for copy in copies:
        copy.start()
    for copy in copies:
        copy.wait()
    count, rows, pts = out_ref.shape
    block = rows - EXTRA
    point = points_ref[...]
    high = point.astype(BF16).astype(F32)
    extra_ref[...] = jnp.zeros_like(extra_ref)
    extra_ref[0:3, :] = high
    extra_ref[3:4, 0 : mask_ref.shape[1]] = mask_ref[...].astype(F32)
    extra_ref[4:7, :] = point - high
    turned = iterate_ref[...].astype(F32).T.astype(BF16)
    extra = extra_ref[...].astype(BF16)
    for dest in range(count):
        part = dest % CELL
        out_ref[dest, 0:block, :] = turned[part * block : (part + 1) * block]
        out_ref[dest, block:rows, :] = extra


def near_kernel(cell_ref, recv_ref, inverse_ref, out_ref, kept_ref, acc_ref, left_ref, sem_ref):
    fetch = pltpu.make_async_copy(inverse_ref, kept_ref, sem_ref)
    fetch.start()
    count, rows, pts = recv_ref.shape
    block = rows - EXTRA
    first = cell_ref[0]
    row_no = lax.broadcasted_iota(jnp.int32, (EXTRA, pts), 0)
    coord_rows = (row_no % 4) != 3
    three_rows = row_no < 3
    ones = jnp.where(three_rows, 1.0, 0.0)

    def coords(extra):
        whole = jnp.where(coord_rows, extra + pltpu.roll(extra, 4, 0), 0.0)
        square = jnp.sum(jnp.where(three_rows, whole * whole, 0.0), axis=0, keepdims=True)
        return whole, square

    def rows_of(parts):
        high, mid, low = parts
        picked = jnp.where(row_no == 1, mid, low)
        return jnp.where(three_rows, jnp.where(row_no == 0, high, picked), 0.0)

    left = []
    cell_rows = lax.broadcasted_iota(jnp.int32, (CELL, pts), 0)
    tile_no = lax.broadcasted_iota(jnp.int32, (CELL, pts), 1)
    masks = jnp.zeros((CELL, pts), F32)
    for member in range(CELL):
        extra = recv_ref[first + member, block:rows, :].astype(F32)
        masks = jnp.where(cell_rows == member, extra[3:4, :], masks)
        whole, square = coords(extra)
        parts = split_parts(2.0 * EXP2_COEF * whole)
        own = split_parts(EXP2_BASE - EXP2_COEF * square)
        unit = jnp.where(cell_rows == member, 1.0, 0.0)
        value = jnp.concatenate([*parts, rows_of(own), ones, unit], axis=0).astype(BF16)
        left_ref[:, member * pts : (member + 1) * pts] = value
    acc_ref[...] = jnp.zeros_like(acc_ref)

    def step(tile, carry):
        extra = recv_ref[tile, block:rows, :].astype(F32)
        whole, square = coords(extra)
        tail = rows_of(split_parts(-EXP2_COEF * square))
        flag = jnp.sum(jnp.where(tile_no == tile, masks, 0.0), axis=1, keepdims=True)
        bias = jnp.broadcast_to((flag - 1.0) * OFF_BIAS, masks.shape)
        right = jnp.concatenate([extra, extra, extra, ones, tail, bias], axis=0).astype(BF16)
        iterate = recv_ref[tile, 0:block, :]
        for low in range(0, CELL * pts, CHUNK):
            span = slice(low, low + CHUNK)
            value = jnp.exp2(dot_tn(right, left_ref[:, span])).astype(BF16)
            acc_ref[:, span] += dot_nn(iterate, value)
        return carry

    lax.fori_loop(0, count, step, 0, unroll=2)
    for member in range(CELL):
        out_ref[member] = acc_ref[:, member * pts : (member + 1) * pts].astype(BF16)
    fetch.wait()


def send_field(field, out_ref):
    turned = field.T.astype(BF16)
    out_ref[...] = turned.reshape(out_ref.shape)


def leaf_kernel(near_ref, right_ref, iterate_ref, inverse_ref, field_ref, out_ref):
    parts, block, pts = near_ref.shape
    near = near_ref[...].reshape(parts * block, pts).astype(F32).T
    resid = right_ref[...] - shift_value * iterate_ref[...].astype(F32) - near
    field = dot_nn(inverse_ref[0], resid.astype(BF16))
    field_ref[...] = field
    send_field(field, out_ref)


def equal_rows(count, value, kind):
    row_no = lax.broadcasted_iota(jnp.int32, (count, value.shape[1]), 0)
    return jnp.where(row_no == value, 1.0, 0.0).astype(kind)


def pick_rows(field, index):
    tiles, cols, pts = field.shape
    tile_of = index // pts
    chosen = equal_rows(pts, index - tile_of * pts, BF16)
    lanes = dot_nn(field.reshape(tiles * cols, pts), chosen)
    total = jnp.zeros((cols, index.shape[1]), F32)
    for tile in range(tiles):
        total = total + jnp.where(tile_of == tile, lanes[tile * cols : (tile + 1) * cols], 0.0)
    return total


def store_copies(value, out_ref):
    if len(out_ref.shape) == 2:
        out_ref[...] = value
    else:
        for copy in range(out_ref.shape[0]):
            out_ref[copy] = value


def pick_kernel(recv_ref, skeleton_ref, *out_refs):
    for level_no in range(LEVELS):
        out_refs[level_no][...] = pick_rows(recv_ref[...], skeleton_ref[level_no]).astype(BF16)


def plan_kernel(tiles, tile_ref, skeleton_ref, lift_ref, rows_ref, slot_ref, over_ref):
    pts = lift_ref.shape[1]
    row_no = lax.broadcasted_iota(jnp.int32, (pts, pts), 0)
    lane_no = lax.broadcasted_iota(jnp.int32, (pts, pts), 1)
    before = jnp.where(row_no < lane_no, 1.0, 0.0).astype(BF16)
    own = lax.broadcasted_iota(jnp.int32, (tiles, pts), 0) == tile_ref[0]
    room_no = lax.broadcasted_iota(jnp.int32, (ROOM, pts), 0).astype(F32)
    most = jnp.zeros((tiles, pts), F32)
    spot = 0
    for level_no in range(1, LEVELS):
        index = skeleton_ref[level_no]
        tile_of = index // pts
        inner = equal_rows(pts, index - tile_of * pts, BF16)
        member = equal_rows(tiles, tile_of, F32)
        present = dot_nt(member.astype(BF16), inner)
        rank = dot_nn(present.astype(BF16), before)
        ranks = jnp.sum(member * dot_nn(rank.astype(BF16), inner), axis=0, keepdims=True)
        slot_ref[level_no - 1] = tile_of * ROOM + ranks.astype(jnp.int32)
        most = jnp.maximum(most, rank + present)
        own_present = jnp.sum(jnp.where(own, present, 0.0), axis=0, keepdims=True)
        own_rank = jnp.sum(jnp.where(own, rank, 0.0), axis=0, keepdims=True)
        chosen = jnp.where((room_no == own_rank) & (own_present > 0.5), 1.0, 0.0).astype(BF16)
        for earlier in range(level_no):
            rows_ref[spot * ROOM : (spot + 1) * ROOM] = dot_nn(chosen, lift_ref[earlier]).astype(BF16)
            spot += 1
    over_ref[0] = (jnp.max(most) > ROOM).astype(jnp.int32)


def fast_kernel(level_no, picked_ref, slot_ref, *refs):
    answer_refs, row_refs, out_ref = refs[:level_no], refs[level_no:-1], refs[-1]
    tiles, room, count = row_refs[0].shape
    total = jnp.zeros((answer_refs[0].shape[0], tiles * room), F32)
    for answer_ref, row_ref in zip(answer_refs, row_refs):
        total = total + dot_nt(answer_ref[...], row_ref[...].reshape(tiles * room, count))
    high = total.astype(BF16)
    low = (total - high.astype(F32)).astype(BF16)
    chosen = equal_rows(tiles * room, slot_ref[level_no - 1], BF16)
    change = dot_nn(high, chosen) + dot_nn(low, chosen)
    store_copies((picked_ref[...].astype(F32) - change).astype(BF16), out_ref)


def copy_kernel(*refs):
    share = refs[0].shape[0]
    for spot, value_ref in enumerate(refs[:-1]):
        for copy in range(refs[-1].shape[0]):
            refs[-1][copy, spot * share : (spot + 1) * share, :] = value_ref[...]


def tile_kernel(lift_ref, answer_ref, out_ref):
    blocks, rows, count = answer_ref.shape
    share = out_ref.shape[1]
    total = jnp.zeros((lift_ref.shape[1], blocks * share), F32)
    for earlier in range(rows // share):
        answer = answer_ref[:, earlier * share : (earlier + 1) * share, :]
        total = total + dot_nt(lift_ref[earlier], answer.reshape(blocks * share, count))
    send_field(total, out_ref)


def less_kernel(level_no, picked_ref, recv_ref, skeleton_ref, out_ref):
    change = pick_rows(recv_ref[...], skeleton_ref[level_no])
    store_copies((picked_ref[...].astype(F32) - change).astype(BF16), out_ref)


def solve_kernel(level_no, leaf_ref, nodes_ref, coupling_ref, inverse_ref, *refs):
    half = nodes_ref.shape[0] // 2
    low = nodes_ref[0].astype(F32)
    high = nodes_ref[half].astype(F32)
    for member in range(1, half):
        low = low + nodes_ref[member].astype(F32)
        high = high + nodes_ref[half + member].astype(F32)
    upper = ((leaf_ref[0] >> level_no) & 1) == 1
    own = jnp.where(upper, high, low)
    other = jnp.where(upper, low, high)
    rhs = own - dot_nt(other.astype(BF16), coupling_ref[0, 0])
    answer = dot_nt(rhs.astype(BF16), inverse_ref[0, 0]).astype(BF16)
    share = answer.shape[0]
    earlier, out_ref = refs[:-1], refs[-1]
    for spot, value_ref in enumerate(earlier):
        out_ref[spot * share : (spot + 1) * share] = value_ref[...]
    out_ref[len(earlier) * share : (len(earlier) + 1) * share] = answer


def lift_kernel(field_ref, lift_ref, answer_ref, out_ref):
    blocks, rows, count = answer_ref.shape
    share = rows // LEVELS
    field = field_ref[...]
    for level_no in range(LEVELS):
        answer = answer_ref[:, level_no * share : (level_no + 1) * share, :]
        field = field - dot_nt(lift_ref[level_no], answer.reshape(blocks * share, count))
    out_ref[...] = field


def level_spec(shape, level_no):
    tail = (0,) * (len(shape) - 1)
    return pl.BlockSpec((1,) + tuple(shape[1:]), lambda step: (level_no,) + tail)


def whole_spec(shape):
    zeros = (0,) * len(shape)
    return pl.BlockSpec(tuple(shape), lambda step: zeros)


def on_device(
    points, iterate, right_side, near_mask, leaf_inverse, skeleton, coupling, reduced_inverse, lift
):
    blk_count = lax.axis_size("blk")
    leaf_count = lax.axis_size("leaf")
    pts, cols = iterate.shape
    slots = skeleton.shape[2]
    share = cols // blk_count
    block = cols // CELL
    leaf_no = lax.axis_index("leaf").astype(jnp.int32).reshape(1)
    first = (lax.axis_index("blk") // CELL * CELL).astype(jnp.int32).reshape(1)
    tile_no = lax.axis_index("blk").astype(jnp.int32).reshape(1)
    cells = [list(range(c, c + CELL)) for c in range(0, blk_count, CELL)]
    leaf_no, first, tile_no, points, skeleton = lax.optimization_barrier(
        (leaf_no, first, tile_no, points, skeleton)
    )

    pairs = LEVELS * (LEVELS - 1) // 2
    rows, slot_of, over = pl.pallas_call(
        lambda *refs: plan_kernel(blk_count, *refs),
        out_shape=(
            jax.ShapeDtypeStruct((pairs * ROOM, slots), BF16),
            jax.ShapeDtypeStruct((LEVELS - 1, 1, slots), jnp.int32),
            jax.ShapeDtypeStruct((1,), jnp.int32),
        ),
        in_specs=[SMEM, VMEM, VMEM],
        out_specs=(VMEM, VMEM, SMEM),
        compiler_params=PARAMS,
        name="plan",
    )(tile_no, skeleton, lift)
    rows = lax.all_gather(rows, "blk", axis=0)
    packed = pl.pallas_call(
        pack_kernel,
        out_shape=jax.ShapeDtypeStruct((blk_count, block + EXTRA, pts), BF16),
        in_specs=[ANY] * 3,
        out_specs=VMEM,
        scratch_shapes=[
            pltpu.VMEM((EXTRA, pts), F32),
            pltpu.VMEM(points.shape, points.dtype),
            pltpu.VMEM(iterate.shape, iterate.dtype),
            pltpu.VMEM(near_mask.shape, near_mask.dtype),
            pltpu.SemaphoreType.DMA((3,)),
        ],
        compiler_params=PARAMS,
        name="pack",
    )(points, iterate, near_mask)
    packed = lax.all_to_all(packed, "blk", 0, 0)
    near, inverse = pl.pallas_call(
        near_kernel,
        out_shape=(
            jax.ShapeDtypeStruct((CELL, block, pts), BF16),
            jax.ShapeDtypeStruct(leaf_inverse.shape, leaf_inverse.dtype),
        ),
        in_specs=[SMEM, VMEM, ANY],
        out_specs=(VMEM, VMEM),
        scratch_shapes=[
            pltpu.VMEM((block, CELL * pts), F32),
            pltpu.VMEM((5 * EXTRA + CELL, CELL * pts), BF16),
            pltpu.SemaphoreType.DMA,
        ],
        compiler_params=PARAMS,
        name="near",
    )(first, packed, leaf_inverse)
    near = lax.all_to_all(near, "blk", 0, 0, axis_index_groups=cells)
    field_shape = jax.ShapeDtypeStruct((pts, cols), F32)
    send_shape = jax.ShapeDtypeStruct((blk_count, share, pts), BF16)
    field, sent = pl.pallas_call(
        leaf_kernel,
        out_shape=(field_shape, send_shape),
        in_specs=[VMEM] * 4,
        out_specs=(VMEM, VMEM),
        compiler_params=PARAMS,
        name="leaf",
    )(near, right_side, iterate, inverse)

    sent = lax.all_to_all(sent, "blk", 0, 0)
    sent, over = lax.optimization_barrier((sent, over))
    small_shape = jax.ShapeDtypeStruct((share, slots), BF16)
    picked = pl.pallas_call(
        pick_kernel,
        out_shape=(small_shape,) * LEVELS,
        in_specs=[VMEM] * 2,
        out_specs=(VMEM,) * LEVELS,
        compiler_params=PARAMS,
        name="pick",
    )(sent, skeleton)

    def fast(level_no, shape, answers):
        offset = level_no * (level_no - 1) // 2
        return pl.pallas_call(
            lambda *refs: fast_kernel(level_no, *refs),
            out_shape=shape,
            grid=(1,),
            in_specs=[whole_spec((share, slots)), whole_spec(slot_of.shape)]
            + [whole_spec((share, slots))] * level_no
            + [
                pl.BlockSpec((blk_count, ROOM, slots), lambda step, spot=offset + k: (0, spot, 0))
                for k in range(level_no)
            ],
            out_specs=whole_spec(shape.shape),
            compiler_params=PARAMS,
            name="fast",
        )(picked[level_no], slot_of, *answers, *[rows] * level_no)

    def slow(level_no, shape, answers):
        copies = pl.pallas_call(
            copy_kernel,
            out_shape=jax.ShapeDtypeStruct((blk_count, level_no * share, slots), BF16),
            in_specs=[VMEM] * level_no,
            out_specs=VMEM,
            compiler_params=PARAMS,
            name="copies",
        )(*answers)
        copies = lax.all_to_all(copies, "blk", 0, 0)
        change = pl.pallas_call(
            tile_kernel,
            out_shape=send_shape,
            in_specs=[VMEM] * 2,
            out_specs=VMEM,
            compiler_params=PARAMS,
            name="tile",
        )(lift, copies)
        change = lax.all_to_all(change, "blk", 0, 0)
        return pl.pallas_call(
            lambda *refs: less_kernel(level_no, *refs),
            out_shape=shape,
            in_specs=[VMEM] * 3,
            out_specs=VMEM,
            compiler_params=PARAMS,
            name="less",
        )(picked[level_no], change, skeleton)

    answers = []
    for level_no in range(LEVELS):
        last = level_no == LEVELS - 1
        width = 2 << level_no
        groups = [list(range(c, c + width)) for c in range(0, leaf_count, width)]
        spread = level_no == 2
        node_shape = (width, share, slots)
        if level_no == 0:
            nodes = picked[0]
        else:
            pick_shape = jax.ShapeDtypeStruct(node_shape if spread else node_shape[1:], BF16)
            nodes = lax.cond(
                over[0] > 0,
                lambda *given, level_no=level_no: slow(level_no, pick_shape, given),
                lambda *given, level_no=level_no: fast(level_no, pick_shape, given),
                *answers,
            )
        if spread:
            nodes = lax.all_to_all(nodes, "leaf", 0, 0, axis_index_groups=groups)
        else:
            nodes = lax.all_gather(nodes, "leaf", axis=0, axis_index_groups=groups)
        earlier = answers if last else []
        answer_shape = ((len(earlier) + 1) * share, slots)
        answer = pl.pallas_call(
            lambda *refs, level_no=level_no: solve_kernel(level_no, *refs),
            out_shape=jax.ShapeDtypeStruct(answer_shape, BF16),
            grid=(1,),
            in_specs=[
                SMEM,
                whole_spec(node_shape),
                level_spec(coupling.shape, level_no),
                level_spec(reduced_inverse.shape, level_no),
            ]
            + [whole_spec((share, slots))] * len(earlier),
            out_specs=whole_spec(answer_shape),
            compiler_params=PARAMS,
            name="solve",
        )(leaf_no, nodes, coupling, reduced_inverse, *earlier)
        answers.append(answer)
    answer = lax.all_gather(answers[-1], "blk", axis=0)
    return pl.pallas_call(
        lift_kernel,
        out_shape=field_shape,
        in_specs=[VMEM] * 3,
        out_specs=VMEM,
        compiler_params=PARAMS,
        name="lift",
    )(field, lift, answer)


def solution(mesh):
    in_specs = (
        P(None, ("leaf", "blk")),
        P(("leaf", "blk"), None),
        P(("leaf", "blk"), None),
        P(("leaf", "blk"), None),
        P(("leaf", "blk"), None, None),
        P(None, "leaf", None),
        P(None, "leaf", None, None),
        P(None, "leaf", None, None),
        P(None, ("leaf", "blk"), None),
    )
    out_specs = P(("leaf", "blk"), None)
    return jax.shard_map(
        on_device, mesh=mesh, in_specs=in_specs, out_specs=out_specs, check_vma=False
    )
```
